32 devices in a mesh: freq: 4 (over x, core), tile: 8 (over z, y).
Axes of the slice: x: 2, y: 2, z: 4, core: 2. Of those that a mesh axis runs over, the one named last changes fastest.
Arguments:
- plus_time: bfloat16 [128, 128, 12288], P('freq', None, 'tile'), may hold values from -6 to 6
- minus_time: bfloat16 [128, 128, 12288], P('freq', None, 'tile'), may hold values from -6 to 6
- gate_starts: int32 [128, 48], P('freq', 'tile'), may hold values from 0 to 64
- tile_ranks: int32 [4, 48, 48], P('freq', None, 'tile'), may hold values from 1 to 64, as said below
- u_factors: bfloat16 [4, 48, 48, 2, 64, 256], P('freq', 'tile'), may hold values from -0.109375 to 0.109375
- v_factors: bfloat16 [4, 48, 48, 2, 64, 256], P('freq', None, 'tile'), may hold values from -0.375 to 0.375
Outputs:
- minus_new: bfloat16 [4, 2, 128, 12288], P('freq', None, None, 'tile')
- plus_new: bfloat16 [4, 2, 128, 12288], P('freq', None, None, 'tile')
- cross_gram: float32 [4, 2, 128, 128], P('freq', None, 'tile')
- normal_gram: float32 [4, 2, 128, 128], P('freq', None, 'tile')
The draws below stay inside these ranges and needn't reach their ends.
Inputs may be any that keep to these rules, and one draw needn't show every extreme that they name: `tile_ranks`: tiles with |i - j| <= 1 have rank 64; every other tile has rank at most 32, and some tile of every draw has exactly 32.
All inputs are finite; a program needn't handle non-finite values.
Results may differ from the reference program's by a relative error of at most 0.014.
Values may be sent and summed in bfloat16 or wider, within the bound.
A program may use at most 192 MiB of HBM per device.

```python
import math
import jax
import jax.numpy as jnp
from jax import lax

S = 128
R = 12288
TILE = 256
KMAX = 64
GATE = 64
NSAMP = 128
NT = 48
F = 4


def draw_tile_ranks(key, part):
    base_ranks = jax.random.randint(jax.random.fold_in(key, 11), (F, NT, NT), KMAX // 4, KMAX // 2 + 1)
    row_ids = lax.broadcasted_iota(jnp.int32, (F, NT, NT), 1)
    col_ids = lax.broadcasted_iota(jnp.int32, (F, NT, NT), 2)
    near_diag = jnp.abs(row_ids - col_ids) <= 1
    corner = (row_ids == 0) & (col_ids == NT - 1)
    base_ranks = jnp.where(corner, KMAX // 2, base_ranks)
    return jnp.where(near_diag, KMAX, base_ranks).astype(jnp.int32)


def set_ends(result, key, smallest, largest):
    place = [jax.random.randint(jax.random.fold_in(key, axis), (), 0, length) for axis, length in enumerate(result.shape)]
    main_axis = result.shape.index(max(result.shape))
    neighbour = place[:main_axis] + [(place[main_axis] + 1) % result.shape[main_axis]] + place[main_axis + 1:]
    return result.at[tuple(place)].set(smallest).at[tuple(neighbour)].set(largest)


def block_scale(stream_key, shape, shards, low, high):
    gain, own = 1.0, jax.random.fold_in(stream_key, 6)
    for axis_at, shards_of in shards:
        draws = jnp.exp(jax.random.uniform(jax.random.fold_in(own, axis_at), (shards_of,), jnp.float32, low / len(shards), high / len(shards)))
        gain = gain * jnp.repeat(draws, shape[axis_at] // shards_of).reshape([-1 if axis == axis_at else 1 for axis in range(len(shape))])
    return gain


def scatter_about(rng, dims, width, bound, cuts=(), kind=jnp.bfloat16):
    level = block_scale(rng, dims, cuts, -0.22, 0.18) if cuts else 1.0
    values = jax.random.normal(rng, dims, jnp.float32) * width * level
    return jnp.minimum(jnp.maximum(values, -bound), bound).astype(kind)


def setup_inputs(seed: int = 0) -> dict:
    arg_keys = jax.random.split(jax.random.key(seed), 7)
    plus_time = scatter_about(arg_keys[0], (S, NSAMP, R), 1.0, 6.0, ((0, 4), (2, 8)))
    minus_time = scatter_about(arg_keys[1], (S, NSAMP, R), 1.0, 6.0, ((0, 4), (2, 8)))
    gate_starts = set_ends(jax.random.randint(arg_keys[2], (S, NT), 0, NSAMP - GATE + 1), jax.random.fold_in(arg_keys[2], 1), 0, NSAMP - GATE).astype(jnp.int32)
    tile_ranks = draw_tile_ranks(jax.random.fold_in(arg_keys[6], 71), 0)
    u_factors = scatter_about(arg_keys[4], (F, NT, NT, 2, KMAX, TILE), (NT * KMAX) ** -0.5, 0.109375, ((0, 4), (1, 8)))
    v_factors = scatter_about(arg_keys[5], (F, NT, NT, 2, KMAX, TILE), TILE ** -0.5, 0.375, ((0, 4), (2, 8)))
    return dict(plus_time=plus_time, minus_time=minus_time, gate_starts=gate_starts, tile_ranks=tile_ranks, u_factors=u_factors, v_factors=v_factors)


def make_table(freq_count, sample_count):
    freq_ids = lax.broadcasted_iota(jnp.int32, (freq_count, sample_count), 0)
    sample_ids = lax.broadcasted_iota(jnp.int32, (freq_count, sample_count), 1)
    phase_ids = freq_ids * sample_ids % sample_count
    angles = phase_ids.astype(jnp.float32) * (2.0 * math.pi / sample_count)
    amplitude = 1.0 / math.sqrt(GATE)
    return jnp.stack([jnp.cos(angles) * amplitude, -jnp.sin(angles) * amplitude]).astype(jnp.bfloat16)

def half_signs(entry_count):
    entry_ids = lax.broadcasted_iota(jnp.int32, (entry_count,), 0)
    return jnp.where(entry_ids < entry_count // 2, 1.0, -1.0).astype(jnp.float32)

def reference(plus_time, minus_time, gate_starts, tile_ranks, u_factors, v_factors):
    tile_count = R // TILE
    dft_table = make_table(F, NSAMP)
    flat_table = dft_table.reshape(2 * F, NSAMP)

    def one_source(src_items):
        plus_row, minus_row, gate_row = src_items
        starts = jnp.repeat(gate_row, TILE)[None, :]
        sample_ids = jnp.arange(NSAMP, dtype=jnp.int32)[:, None]
        inside = (sample_ids >= starts) & (sample_ids < starts + GATE)
        zero_val = jnp.zeros((), plus_row.dtype)
        plus_spec = jnp.dot(flat_table, jnp.where(inside, plus_row, zero_val), preferred_element_type=jnp.float32)
        minus_spec = jnp.dot(flat_table, jnp.where(inside, minus_row, zero_val), preferred_element_type=jnp.float32)
        return jnp.stack([plus_spec, minus_spec]).reshape(2, 2, F, R)
    per_source = lax.map(one_source, (plus_time, minus_time, gate_starts))
    spectra = jnp.transpose(per_source, (3, 2, 1, 0, 4)).astype(jnp.bfloat16)
    sign_vec = half_signs(2 * S)
    rank_ids = jnp.arange(KMAX, dtype=jnp.int32)

    def one_freq(freq_items):
        spec_freq, u_freq, v_freq, rank_freq = freq_items
        columns = spec_freq.reshape(2, 2 * S, tile_count, TILE).astype(jnp.float32)

        def one_row(row_items):
            u_row, v_row, ranks_row = row_items
            partial_c = jnp.einsum('jckr,dsjr->jcdks', v_row.astype(jnp.float32), columns, precision=lax.Precision.HIGHEST)
            coeff_real = partial_c[:, 0, 0] - sign_vec * partial_c[:, 1, 1]
            coeff_imag = partial_c[:, 0, 1] + sign_vec * partial_c[:, 1, 0]
            rank_mask = (rank_ids[None, :] < ranks_row[:, None]).astype(jnp.float32)[:, :, None]
            coeff_all = jnp.stack([coeff_real * rank_mask, coeff_imag * rank_mask], 1).astype(jnp.bfloat16)
            products = jnp.einsum('jckr,jeks->cesr', u_row.astype(jnp.float32), coeff_all.astype(jnp.float32), precision=lax.Precision.HIGHEST)
            resp_real = products[0, 0] - sign_vec[:, None] * products[1, 1]
            resp_imag = products[0, 1] + sign_vec[:, None] * products[1, 0]
            return jnp.stack([resp_real, resp_imag])
        rows_out = lax.map(one_row, (u_freq, v_freq, rank_freq))
        return jnp.transpose(rows_out, (1, 2, 0, 3)).reshape(2, 2 * S, R)
    response = lax.map(one_freq, (spectra, u_factors, v_factors, tile_ranks))
    rounded = response.astype(jnp.bfloat16)
    minus_new = rounded[:, :, :S]
    plus_new = rounded[:, :, S:]
    gram_parts = jnp.einsum('fczr,fesr->fczes', rounded.astype(jnp.float32), plus_new.astype(jnp.float32), precision=lax.Precision.HIGHEST)
    gram_real = gram_parts[:, 0, :, 0] + gram_parts[:, 1, :, 1]
    gram_imag = gram_parts[:, 1, :, 0] - gram_parts[:, 0, :, 1]
    cross_gram = jnp.stack([gram_real[:, :S], gram_imag[:, :S]], 1) / math.sqrt(R)
    normal_gram = jnp.stack([gram_real[:, S:], gram_imag[:, S:]], 1) / R
    return (minus_new, plus_new, cross_gram, normal_gram)
```

```python
import functools
import math

import jax
import jax.numpy as jnp
from jax import lax
from jax.experimental import pallas as pl
from jax.experimental.pallas import tpu as pltpu
from jax.sharding import PartitionSpec as P

GATE = 64
MESH = pl.DeviceIdType.MESH
NT_DIMS = (((1,), (1,)), ((), ()))
TN_DIMS = (((0,), (0,)), ((), ()))


def make_table(freq_count, sample_count):
    freq_ids = lax.broadcasted_iota(jnp.int32, (freq_count, sample_count), 0)
    sample_ids = lax.broadcasted_iota(jnp.int32, (freq_count, sample_count), 1)
    phase_ids = freq_ids * sample_ids % sample_count
    angles = phase_ids.astype(jnp.float32) * (2.0 * math.pi / sample_count)
    amplitude = 1.0 / math.sqrt(GATE)
    return jnp.stack([jnp.cos(angles) * amplitude, -jnp.sin(angles) * amplitude]).astype(
        jnp.bfloat16
    )


def spectra_kernel(starts, table, plus, minus, out):
    block, tile = pl.program_id(0), pl.program_id(1)
    freqs, _, _, sources, width = out.shape
    samples = plus.shape[1]
    shape = (2 * freqs, sources, 2 * samples)
    rows = 2 * freqs * sources
    row_source = lax.broadcasted_iota(jnp.int32, shape, 1).reshape(rows, 2 * samples)
    column = lax.broadcasted_iota(jnp.int32, (rows, 2 * samples), 1)
    second = column >= samples
    sample = jnp.where(second, column - samples, column)
    row_source = row_source - second.astype(jnp.int32)
    values = table[...]
    total_plus = jnp.zeros((rows, width), jnp.float32)
    total_minus = jnp.zeros((rows, width), jnp.float32)
    for pair in range(sources // 2):
        first_id = block * sources + 2 * pair
        start = jnp.where(second, starts[first_id + 1, tile], starts[first_id, tile])
        inside = (sample >= start) & (sample < start + GATE) & (row_source == 2 * pair)
        gated = jnp.where(inside, values, 0.0).astype(jnp.bfloat16)
        both = slice(2 * pair, 2 * pair + 2)
        total_plus += jnp.dot(
            gated, plus[both].reshape(2 * samples, width), preferred_element_type=jnp.float32
        )
        total_minus += jnp.dot(
            gated, minus[both].reshape(2 * samples, width), preferred_element_type=jnp.float32
        )
    out[:, :, 0] = total_plus.reshape(freqs, 2, sources, width).astype(out.dtype)
    out[:, :, 1] = total_minus.reshape(freqs, 2, sources, width).astype(out.dtype)


def local_spectra(plus_time, minus_time, gate_starts, freq_total):
    sources, samples, receivers = plus_time.shape
    tiles = gate_starts.shape[1]
    width = receivers // tiles
    block = math.gcd(16, sources)
    table = make_table(freq_total, samples).transpose(1, 0, 2).astype(jnp.float32)
    table = jnp.broadcast_to(table[:, :, None, None], (freq_total, 2, block, 2, samples))
    table = table.reshape(freq_total * 2 * block, 2 * samples)
    return pl.pallas_call(
        spectra_kernel,
        grid=(sources // block, tiles),
        in_specs=[
            pl.BlockSpec(memory_space=pltpu.SMEM),
            pl.BlockSpec(table.shape, lambda b, j: (0, 0)),
            pl.BlockSpec((block, samples, width), lambda b, j: (b, 0, j)),
            pl.BlockSpec((block, samples, width), lambda b, j: (b, 0, j)),
        ],
        out_specs=pl.BlockSpec((freq_total, 2, 2, block, width), lambda b, j: (0, 0, 0, b, j)),
        out_shape=jax.ShapeDtypeStruct((freq_total, 2, 2, sources, receivers), jnp.bfloat16),
        name="gated_spectra",
    )(gate_starts, table, plus_time, minus_time)


def partner(me, step):
    other, bit = me, 1
    while bit <= step:
        if step & bit:
            other = other + bit - 2 * bit * ((me // bit) % 2)
        bit *= 2
    return other


def swapped(block, count, axis):
    parts = [lax.slice_in_dim(block, n * count, (n + 1) * count, axis=axis) for n in range(4)]
    return jnp.concatenate([-parts[2], parts[3], parts[0], -parts[1]], axis=axis)


def operator_kernel(
    n, nf, ranks, spec, u_hbm, v_hbm, minus, plus, cross, normal,
    xall, v_s, u_s, vb, ub, send, recv, cband, bin_, acc, gsum, gsend, grecv,
    sem_v, sem_u, sem_vb, sem_ub, fsend, frecv, csend, crecv, bsend, brecv, gs_sem, gr_sem,
):
    me = lax.axis_index("tile")
    mf = lax.axis_index("freq")
    tiles, half, width = v_s.shape[0], v_s.shape[3], v_s.shape[4]
    sl = spec.shape[3]
    count = sl * nf
    lanes = 4 * count
    base = me * tiles
    total_tiles = n * tiles
    first = 1 - (me + n - 1) // n
    last = (me + 1) // n

    def load_v(j):
        return pltpu.make_async_copy(
            v_hbm.at[0, :, j, :, pl.ds(0, half), :], v_s.at[j], sem_v.at[j]
        )

    def load_u(m):
        src = partner(me, m)
        return pltpu.make_async_copy(
            u_hbm.at[0, :, pl.ds(src * tiles, tiles), :, pl.ds(0, half), :], u_s.at[m], sem_u.at[m]
        )

    def load_band(o, j, right):
        row, col = base + j + o - 1, base + j - o + 1
        if j + o - 1 < 0:
            row = row + first
        if j + o - 1 >= tiles:
            row = row - last
        if j - o + 1 < 0:
            col = col + first
        if j - o + 1 >= tiles:
            col = col - last
        if right:
            return pltpu.make_async_copy(
                v_hbm.at[0, row, j, :, pl.ds(half, half), :], vb.at[o, j], sem_vb.at[o, j]
            )
        return pltpu.make_async_copy(
            u_hbm.at[0, j, col, :, pl.ds(half, half), :], ub.at[o, j], sem_ub.at[o, j]
        )

    def columns(j):
        return pl.ds(pl.multiple_of(j * width, width), width)

    def freq_copy(g, j):
        peer = partner(mf, g)
        return pltpu.make_async_remote_copy(
            src_ref=spec.at[peer, :, :, :, columns(j)],
            dst_ref=xall.at[:, :, pl.ds(pl.multiple_of(mf * sl, sl), sl), columns(j)],
            send_sem=fsend.at[g, j],
            recv_sem=frecv.at[g, j],
            device_id={"freq": peer},
            device_id_type=MESH,
        )

    def coeff_copy(m, j):
        return pltpu.make_async_remote_copy(
            src_ref=send.at[j, m],
            dst_ref=recv.at[j, m],
            send_sem=csend.at[m, j],
            recv_sem=crecv.at[m, j],
            device_id={"tile": partner(me, m)},
            device_id_type=MESH,
        )

    def band_copy(side):
        source = cband.at[2, tiles + 1] if side == 0 else cband.at[0, 0]
        target = lax.rem(me + 1, n) if side == 0 else lax.rem(me + n - 1, n)
        return pltpu.make_async_remote_copy(
            src_ref=source,
            dst_ref=bin_.at[side],
            send_sem=bsend.at[side],
            recv_sem=brecv.at[side],
            device_id={"tile": target},
            device_id_type=MESH,
        )

    def gram_copy(m):
        other = partner(me, m)
        return pltpu.make_async_remote_copy(
            src_ref=gsend.at[other],
            dst_ref=grecv.at[m],
            send_sem=gs_sem.at[m],
            recv_sem=gr_sem.at[m],
            device_id={"tile": other},
            device_id_type=MESH,
        )

    for j in range(tiles):
        load_v(j).start()
        for o in range(3):
            load_band(o, j, True).start()
            load_band(o, j, False).start()
    for m in range(n):
        load_u(m).start()

    barrier = pltpu.get_barrier_semaphore()
    for m in range(1, n):
        pl.semaphore_signal(
            barrier, inc=1, device_id={"tile": partner(me, m)}, device_id_type=MESH
        )
    for g in range(1, nf):
        pl.semaphore_signal(
            barrier, inc=1, device_id={"freq": partner(mf, g)}, device_id_type=MESH
        )
    pl.semaphore_wait(barrier, n + nf - 2)

    for j in range(tiles):
        for g in range(1, nf):
            freq_copy(g, j).start()
    xall[:, :, pl.ds(pl.multiple_of(mf * sl, sl), sl), :] = spec[mf]
    acc[...] = jnp.zeros_like(acc)
    for j in range(tiles):
        for o in range(3):
            load_band(o, j, True).wait()

    rank_id = lax.broadcasted_iota(jnp.int32, (half, lanes), 0)

    def product(a_real, a_imag, b_one, b_two):
        return lax.dot_general(
            a_real, b_one, NT_DIMS, preferred_element_type=jnp.float32
        ) + lax.dot_general(a_imag, b_two, NT_DIMS, preferred_element_type=jnp.float32)

    def coefficients(j, _):
        for g in range(1, nf):
            freq_copy(g, j).wait_recv()
        load_v(j).wait()
        b_one = xall[:, :, :, columns(j)].reshape(lanes, width)
        b_two = swapped(b_one, count, 0)
        for m in list(range(1, n)) + [0]:
            row = partner(me, m) * tiles
            c = product(
                v_s[j, pl.ds(row, tiles), 0].reshape(tiles * half, width),
                v_s[j, pl.ds(row, tiles), 1].reshape(tiles * half, width),
                b_one,
                b_two,
            )
            target = send if m else recv
            for i in range(tiles):
                kept = jnp.where(
                    rank_id < ranks[0, row + i, j], c[i * half : (i + 1) * half], 0.0
                )
                target[j, m, i] = kept.astype(jnp.bfloat16)
            if m:
                coeff_copy(m, j).start()
        c = product(
            vb[:, j, 0].reshape(3 * half, width), vb[:, j, 1].reshape(3 * half, width), b_one, b_two
        ).astype(jnp.bfloat16)
        for o in range(3):
            cband[o, j + o] = c[o * half : (o + 1) * half]
        return 0

    lax.fori_loop(0, tiles, coefficients, 0)
    band_copy(0).start()
    band_copy(1).start()
    for m in range(n):
        load_u(m).wait()
    for j in range(tiles):
        for o in range(3):
            load_band(o, j, False).wait()

    def add(i, c, u_real, u_imag):
        acc[i] += lax.dot_general(
            c, u_real, TN_DIMS, preferred_element_type=jnp.float32
        ) + lax.dot_general(
            swapped(c, count, 1), u_imag, TN_DIMS, preferred_element_type=jnp.float32
        )

    def responses(j, _):
        for m in range(1, n):
            coeff_copy(m, j).wait_recv()

        def one_row(i, _):
            add(
                i,
                recv[j, :, i].reshape(n * half, lanes),
                u_s[:, i, j, 0].reshape(n * half, width),
                u_s[:, i, j, 1].reshape(n * half, width),
            )
            return 0

        return lax.fori_loop(0, tiles, one_row, 0)

    lax.fori_loop(0, tiles - 1, responses, 0)
    band_copy(0).wait_recv()
    band_copy(1).wait_recv()
    zero = jnp.zeros((half, lanes), jnp.bfloat16)
    from_before = jnp.where(first == 0, bin_[0], zero)
    from_after = jnp.where(last == 0, bin_[1], zero)
    for i in range(tiles):
        c = [cband[o, i + 1] for o in range(3)]
        if i == 0:
            c[2] = from_before
        if i == tiles - 1:
            c[0] = from_after
        add(
            i,
            jnp.concatenate(c, axis=0),
            ub[:, i, 0].reshape(3 * half, width),
            ub[:, i, 1].reshape(3 * half, width),
        )
    responses(tiles - 1, 0)

    gsum[...] = jnp.zeros_like(gsum)

    def finish(i, _):
        rounded = acc[i].astype(jnp.bfloat16)
        parts = [rounded[p * count : (p + 1) * count] for p in range(4)]
        for c in range(2):
            minus[0, c, :, columns(i)] = parts[2 * c]
            plus[0, c, :, columns(i)] = parts[2 * c + 1]
        gsum[...] += lax.dot_general(
            rounded,
            jnp.concatenate([parts[1], parts[3]], axis=0),
            NT_DIMS,
            preferred_element_type=jnp.float32,
        )
        return 0

    lax.fori_loop(0, tiles, finish, 0)
    receivers = total_tiles * width
    share = count // n
    for q, scale in enumerate((1.0 / math.sqrt(receivers), 1.0 / receivers)):
        top = slice(q * count, (q + 1) * count)
        low = slice((2 + q) * count, (3 + q) * count)
        real = (gsum[top, :count] + gsum[low, count:]) * scale
        imag = (gsum[low, :count] - gsum[top, count:]) * scale
        for d in range(n):
            gsend[d, q, 0] = real[d * share : (d + 1) * share]
            gsend[d, q, 1] = imag[d * share : (d + 1) * share]
    for m in range(1, n):
        gram_copy(m).start()
    total = gsend[me]
    for m in range(1, n):
        gram_copy(m).wait_recv()
        total = total + grecv[m]
    cross[0] = total[0]
    normal[0] = total[1]

    for j in range(tiles):
        for g in range(1, nf):
            freq_copy(g, j).wait_send()
        for m in range(1, n):
            coeff_copy(m, j).wait_send()
    band_copy(0).wait_send()
    band_copy(1).wait_send()
    for m in range(1, n):
        gram_copy(m).wait_send()


def on_device(n, nf, plus_time, minus_time, gate_starts, tile_ranks, u_factors, v_factors):
    freq_total = u_factors.shape[0] * nf
    tiles = v_factors.shape[2]
    half = v_factors.shape[4] // 2
    width = v_factors.shape[5]
    spec = local_spectra(plus_time, minus_time, gate_starts, freq_total)
    sl, receivers = spec.shape[3], spec.shape[4]
    count = sl * nf
    lanes = 4 * count
    share = count // n
    bf16, f32 = jnp.bfloat16, jnp.float32
    vmem = pl.BlockSpec(memory_space=pltpu.VMEM)
    dma = pltpu.SemaphoreType.DMA
    return pl.pallas_call(
        functools.partial(operator_kernel, n, nf),
        out_shape=(
            jax.ShapeDtypeStruct((1, 2, count, receivers), bf16),
            jax.ShapeDtypeStruct((1, 2, count, receivers), bf16),
            jax.ShapeDtypeStruct((1, 2, share, count), f32),
            jax.ShapeDtypeStruct((1, 2, share, count), f32),
        ),
        in_specs=[
            pl.BlockSpec(memory_space=pltpu.SMEM),
            vmem,
            pl.BlockSpec(memory_space=pl.ANY),
            pl.BlockSpec(memory_space=pl.ANY),
        ],
        out_specs=(vmem, vmem, vmem, vmem),
        scratch_shapes=[
            pltpu.VMEM((2, 2, count, receivers), bf16),
            pltpu.VMEM((tiles, n * tiles, 2, half, width), bf16),
            pltpu.VMEM((n, tiles, tiles, 2, half, width), bf16),
            pltpu.VMEM((3, tiles, 2, half, width), bf16),
            pltpu.VMEM((3, tiles, 2, half, width), bf16),
            pltpu.VMEM((tiles, n, tiles, half, lanes), bf16),
            pltpu.VMEM((tiles, n, tiles, half, lanes), bf16),
            pltpu.VMEM((3, tiles + 2, half, lanes), bf16),
            pltpu.VMEM((2, half, lanes), bf16),
            pltpu.VMEM((tiles, lanes, width), f32),
            pltpu.VMEM((lanes, 2 * count), f32),
            pltpu.VMEM((n, 2, 2, share, count), f32),
            pltpu.VMEM((n, 2, 2, share, count), f32),
            dma((tiles,)),
            dma((n,)),
            dma((3, tiles)),
            dma((3, tiles)),
            dma((nf, tiles)),
            dma((nf, tiles)),
            dma((n, tiles)),
            dma((n, tiles)),
            dma((2,)),
            dma((2,)),
            dma((n,)),
            dma((n,)),
        ],
        compiler_params=pltpu.CompilerParams(
            collective_id=0, has_side_effects=True, vmem_limit_bytes=60 << 20
        ),
        name="reflection_operator",
    )(tile_ranks, spec, u_factors, v_factors)


def solution(mesh):
    placed = (
        P("freq", None, "tile"),
        P("freq", None, "tile"),
        P("freq", "tile"),
        P("freq", None, "tile"),
        P("freq", "tile", None, None, None, None),
        P("freq", None, "tile", None, None, None),
    )
    return jax.shard_map(
        functools.partial(on_device, mesh.shape["tile"], mesh.shape["freq"]),
        mesh=mesh,
        in_specs=placed,
        out_specs=(
            P("freq", None, None, "tile"),
            P("freq", None, None, "tile"),
            P("freq", None, "tile", None),
            P("freq", None, "tile", None),
        ),
        check_vma=False,
    )
```

```python
import functools
import math

import jax
import jax.numpy as jnp
from jax import lax
from jax.experimental import pallas as pl
from jax.experimental.pallas import tpu as pltpu
from jax.sharding import PartitionSpec as P

GATE = 64
MESH = pl.DeviceIdType.MESH
NT_DIMS = (((1,), (1,)), ((), ()))
TN_DIMS = (((0,), (0,)), ((), ()))


def make_table(freq_count, sample_count):
    freq_ids = lax.broadcasted_iota(jnp.int32, (freq_count, sample_count), 0)
    sample_ids = lax.broadcasted_iota(jnp.int32, (freq_count, sample_count), 1)
    phase_ids = freq_ids * sample_ids % sample_count
    angles = phase_ids.astype(jnp.float32) * (2.0 * math.pi / sample_count)
    amplitude = 1.0 / math.sqrt(GATE)
    return jnp.stack([jnp.cos(angles) * amplitude, -jnp.sin(angles) * amplitude]).astype(
        jnp.bfloat16
    )


def spectra_kernel(starts, table, plus, minus, out):
    block, tile = pl.program_id(0), pl.program_id(1)
    freqs, _, _, sources, width = out.shape
    samples = plus.shape[1]
    shape = (2 * freqs, sources, 2 * samples)
    rows = 2 * freqs * sources
    row_source = lax.broadcasted_iota(jnp.int32, shape, 1).reshape(rows, 2 * samples)
    column = lax.broadcasted_iota(jnp.int32, (rows, 2 * samples), 1)
    second = column >= samples
    sample = jnp.where(second, column - samples, column)
    row_source = row_source - second.astype(jnp.int32)
    values = table[...]
    total_plus = jnp.zeros((rows, width), jnp.float32)
    total_minus = jnp.zeros((rows, width), jnp.float32)
    for pair in range(sources // 2):
        first_id = block * sources + 2 * pair
        start = jnp.where(second, starts[first_id + 1, tile], starts[first_id, tile])
        inside = (sample >= start) & (sample < start + GATE) & (row_source == 2 * pair)
        gated = jnp.where(inside, values, 0.0).astype(jnp.bfloat16)
        both = slice(2 * pair, 2 * pair + 2)
        total_plus += jnp.dot(
            gated, plus[both].reshape(2 * samples, width), preferred_element_type=jnp.float32
        )
        total_minus += jnp.dot(
            gated, minus[both].reshape(2 * samples, width), preferred_element_type=jnp.float32
        )
    out[:, :, 0] = total_plus.reshape(freqs, 2, sources, width).astype(out.dtype)
    out[:, :, 1] = total_minus.reshape(freqs, 2, sources, width).astype(out.dtype)


def local_spectra(plus_time, minus_time, gate_starts, freq_total):
    sources, samples, receivers = plus_time.shape
    tiles = gate_starts.shape[1]
    width = receivers // tiles
    block = math.gcd(16, sources)
    table = make_table(freq_total, samples).transpose(1, 0, 2).astype(jnp.float32)
    table = jnp.broadcast_to(table[:, :, None, None], (freq_total, 2, block, 2, samples))
    table = table.reshape(freq_total * 2 * block, 2 * samples)
    return pl.pallas_call(
        spectra_kernel,
        grid=(sources // block, tiles),
        in_specs=[
            pl.BlockSpec(memory_space=pltpu.SMEM),
            pl.BlockSpec(table.shape, lambda b, j: (0, 0)),
            pl.BlockSpec((block, samples, width), lambda b, j: (b, 0, j)),
            pl.BlockSpec((block, samples, width), lambda b, j: (b, 0, j)),
        ],
        out_specs=pl.BlockSpec((freq_total, 2, 2, block, width), lambda b, j: (0, 0, 0, b, j)),
        out_shape=jax.ShapeDtypeStruct((freq_total, 2, 2, sources, receivers), jnp.bfloat16),
        name="gated_spectra",
    )(gate_starts, table, plus_time, minus_time)


def partner(me, step):
    other, bit = me, 1
    while bit <= step:
        if step & bit:
            other = other + bit - 2 * bit * ((me // bit) % 2)
        bit *= 2
    return other


def swapped(block, count, axis):
    parts = [lax.slice_in_dim(block, n * count, (n + 1) * count, axis=axis) for n in range(4)]
    return jnp.concatenate([-parts[2], parts[3], parts[0], -parts[1]], axis=axis)


def operator_kernel(
    n, nf, ranks, spec, u_hbm, v_hbm, minus, plus, cross, normal,
    xall, v_s, u_s, vb, ub, send, recv, cband, bin_, acc, gsum, gsend, grecv,
    sem_v, sem_u, sem_vb, sem_ub, fsend, frecv, csend, crecv, bsend, brecv, gs_sem, gr_sem,
):
    me = lax.axis_index("tile")
    mf = lax.axis_index("freq")
    tiles, half, width = v_s.shape[0], v_s.shape[3], v_s.shape[4]
    sl = spec.shape[3]
    count = sl * nf
    lanes = 4 * count
    base = me * tiles
    total_tiles = n * tiles
    first = 1 - (me + n - 1) // n
    last = (me + 1) // n
    inner = ((me + n // 4) // (n // 2)) % 2

    def load_v(j):
        return pltpu.make_async_copy(
            v_hbm.at[0, :, j, :, pl.ds(0, half), :], v_s.at[j], sem_v.at[j]
        )

    def load_u(m):
        src = partner(me, m)
        return pltpu.make_async_copy(
            u_hbm.at[0, :, pl.ds(src * tiles, tiles), :, pl.ds(0, half), :], u_s.at[m], sem_u.at[m]
        )

    def load_band(o, j, right):
        row, col = base + j + o - 1, base + j - o + 1
        if j + o - 1 < 0:
            row = row + first
        if j + o - 1 >= tiles:
            row = row - last
        if j - o + 1 < 0:
            col = col + first
        if j - o + 1 >= tiles:
            col = col - last
        if right:
            return pltpu.make_async_copy(
                v_hbm.at[0, row, j, :, pl.ds(half, half), :], vb.at[o, j], sem_vb.at[o, j]
            )
        return pltpu.make_async_copy(
            u_hbm.at[0, j, col, :, pl.ds(half, half), :], ub.at[o, j], sem_ub.at[o, j]
        )

    def columns(j):
        return pl.ds(pl.multiple_of(j * width, width), width)

    def freq_copy(g, j):
        peer = partner(mf, g)
        return pltpu.make_async_remote_copy(
            src_ref=spec.at[peer, :, :, :, columns(j)],
            dst_ref=xall.at[:, :, pl.ds(pl.multiple_of(mf * sl, sl), sl), columns(j)],
            send_sem=fsend.at[g, j],
            recv_sem=frecv.at[g, j],
            device_id={"freq": peer},
            device_id_type=MESH,
        )

    def coeff_copy(m, j):
        return pltpu.make_async_remote_copy(
            src_ref=send.at[j, m],
            dst_ref=recv.at[j, m],
            send_sem=csend.at[m, j],
            recv_sem=crecv.at[m, j],
            device_id={"tile": partner(me, m)},
            device_id_type=MESH,
        )

    def band_copy(side):
        source = cband.at[2, tiles + 1] if side == 0 else cband.at[0, 0]
        target = lax.rem(me + 1, n) if side == 0 else lax.rem(me + n - 1, n)
        return pltpu.make_async_remote_copy(
            src_ref=source,
            dst_ref=bin_.at[side],
            send_sem=bsend.at[side],
            recv_sem=brecv.at[side],
            device_id={"tile": target},
            device_id_type=MESH,
        )

    def gram_copy(m):
        other = partner(me, m)
        return pltpu.make_async_remote_copy(
            src_ref=gsend.at[other],
            dst_ref=grecv.at[m],
            send_sem=gs_sem.at[m],
            recv_sem=gr_sem.at[m],
            device_id={"tile": other},
            device_id_type=MESH,
        )

    for j in range(tiles):
        load_v(j).start()
        for o in range(3):
            load_band(o, j, True).start()
            load_band(o, j, False).start()
    for m in range(n):
        load_u(m).start()

    barrier = pltpu.get_barrier_semaphore()
    for m in range(1, n):
        pl.semaphore_signal(
            barrier, inc=1, device_id={"tile": partner(me, m)}, device_id_type=MESH
        )
    for g in range(1, nf):
        pl.semaphore_signal(
            barrier, inc=1, device_id={"freq": partner(mf, g)}, device_id_type=MESH
        )
    pl.semaphore_wait(barrier, n + nf - 2)

    for j in range(tiles):
        for g in range(1, nf):
            freq_copy(g, j).start()
    xall[:, :, pl.ds(pl.multiple_of(mf * sl, sl), sl), :] = spec[mf]
    acc[...] = jnp.zeros_like(acc)
    for j in range(tiles):
        for o in range(3):
            load_band(o, j, True).wait()

    rank_id = lax.broadcasted_iota(jnp.int32, (half, lanes), 0)

    def product(a_real, a_imag, b_one, b_two):
        return lax.dot_general(
            a_real, b_one, NT_DIMS, preferred_element_type=jnp.float32
        ) + lax.dot_general(a_imag, b_two, NT_DIMS, preferred_element_type=jnp.float32)

    def coefficients(j, _):
        for g in range(1, nf):
            freq_copy(g, j).wait_recv()
        load_v(j).wait()
        b_one = xall[:, :, :, columns(j)].reshape(lanes, width)
        b_two = swapped(b_one, count, 0)
        for m in list(range(1, n)) + [0]:
            row = partner(me, m) * tiles
            c = product(
                v_s[j, pl.ds(row, tiles), 0].reshape(tiles * half, width),
                v_s[j, pl.ds(row, tiles), 1].reshape(tiles * half, width),
                b_one,
                b_two,
            )
            target = send if m else recv
            for i in range(tiles):
                kept = jnp.where(
                    rank_id < ranks[0, row + i, j], c[i * half : (i + 1) * half], 0.0
                )
                target[j, m, i] = kept.astype(jnp.bfloat16)
            if 0 < m < n // 2:
                coeff_copy(m, j).start()
            elif m:

                @pl.when(inner == 1)
                def _():
                    coeff_copy(m, j).start()

        c = product(
            vb[:, j, 0].reshape(3 * half, width), vb[:, j, 1].reshape(3 * half, width), b_one, b_two
        ).astype(jnp.bfloat16)
        for o in range(3):
            cband[o, j + o] = c[o * half : (o + 1) * half]
        return 0

    lax.fori_loop(0, tiles, coefficients, 0)

    @pl.when(inner == 0)
    def _():
        for j in range(tiles):
            for m in range(n // 2, n):
                coeff_copy(m, j).start()

    band_copy(0).start()
    band_copy(1).start()
    for m in range(n):
        load_u(m).wait()
    for j in range(tiles):
        for o in range(3):
            load_band(o, j, False).wait()

    def add(i, c, u_real, u_imag):
        acc[i] += lax.dot_general(
            c, u_real, TN_DIMS, preferred_element_type=jnp.float32
        ) + lax.dot_general(
            swapped(c, count, 1), u_imag, TN_DIMS, preferred_element_type=jnp.float32
        )

    def responses(j, _):
        for m in range(1, n):
            coeff_copy(m, j).wait_recv()

        def one_row(i, _):
            add(
                i,
                recv[j, :, i].reshape(n * half, lanes),
                u_s[:, i, j, 0].reshape(n * half, width),
                u_s[:, i, j, 1].reshape(n * half, width),
            )
            return 0

        return lax.fori_loop(0, tiles, one_row, 0)

    lax.fori_loop(0, tiles - 1, responses, 0)
    band_copy(0).wait_recv()
    band_copy(1).wait_recv()
    zero = jnp.zeros((half, lanes), jnp.bfloat16)
    from_before = jnp.where(first == 0, bin_[0], zero)
    from_after = jnp.where(last == 0, bin_[1], zero)
    for i in range(tiles):
        c = [cband[o, i + 1] for o in range(3)]
        if i == 0:
            c[2] = from_before
        if i == tiles - 1:
            c[0] = from_after
        add(
            i,
            jnp.concatenate(c, axis=0),
            ub[:, i, 0].reshape(3 * half, width),
            ub[:, i, 1].reshape(3 * half, width),
        )
    responses(tiles - 1, 0)

    gsum[...] = jnp.zeros_like(gsum)

    def finish(i, _):
        rounded = acc[i].astype(jnp.bfloat16)
        parts = [rounded[p * count : (p + 1) * count] for p in range(4)]
        for c in range(2):
            minus[0, c, :, columns(i)] = parts[2 * c]
            plus[0, c, :, columns(i)] = parts[2 * c + 1]
        gsum[...] += lax.dot_general(
            rounded,
            jnp.concatenate([parts[1], parts[3]], axis=0),
            NT_DIMS,
            preferred_element_type=jnp.float32,
        )
        return 0

    lax.fori_loop(0, tiles, finish, 0)
    receivers = total_tiles * width
    share = count // n
    for q, scale in enumerate((1.0 / math.sqrt(receivers), 1.0 / receivers)):
        top = slice(q * count, (q + 1) * count)
        low = slice((2 + q) * count, (3 + q) * count)
        real = (gsum[top, :count] + gsum[low, count:]) * scale
        imag = (gsum[low, :count] - gsum[top, count:]) * scale
        for d in range(n):
            gsend[d, q, 0] = real[d * share : (d + 1) * share]
            gsend[d, q, 1] = imag[d * share : (d + 1) * share]
    for m in range(1, n):
        gram_copy(m).start()
    total = gsend[me]
    for m in range(1, n):
        gram_copy(m).wait_recv()
        total = total + grecv[m]
    cross[0] = total[0]
    normal[0] = total[1]

    for j in range(tiles):
        for g in range(1, nf):
            freq_copy(g, j).wait_send()
        for m in range(1, n):
            coeff_copy(m, j).wait_send()
    band_copy(0).wait_send()
    band_copy(1).wait_send()
    for m in range(1, n):
        gram_copy(m).wait_send()


def on_device(n, nf, plus_time, minus_time, gate_starts, tile_ranks, u_factors, v_factors):
    freq_total = u_factors.shape[0] * nf
    tiles = v_factors.shape[2]
    half = v_factors.shape[4] // 2
    width = v_factors.shape[5]
    spec = local_spectra(plus_time, minus_time, gate_starts, freq_total)
    sl, receivers = spec.shape[3], spec.shape[4]
    count = sl * nf
    lanes = 4 * count
    share = count // n
    bf16, f32 = jnp.bfloat16, jnp.float32
    vmem = pl.BlockSpec(memory_space=pltpu.VMEM)
    dma = pltpu.SemaphoreType.DMA
    return pl.pallas_call(
        functools.partial(operator_kernel, n, nf),
        out_shape=(
            jax.ShapeDtypeStruct((1, 2, count, receivers), bf16),
            jax.ShapeDtypeStruct((1, 2, count, receivers), bf16),
            jax.ShapeDtypeStruct((1, 2, share, count), f32),
            jax.ShapeDtypeStruct((1, 2, share, count), f32),
        ),
        in_specs=[
            pl.BlockSpec(memory_space=pltpu.SMEM),
            vmem,
            pl.BlockSpec(memory_space=pl.ANY),
            pl.BlockSpec(memory_space=pl.ANY),
        ],
        out_specs=(vmem, vmem, vmem, vmem),
        scratch_shapes=[
            pltpu.VMEM((2, 2, count, receivers), bf16),
            pltpu.VMEM((tiles, n * tiles, 2, half, width), bf16),
            pltpu.VMEM((n, tiles, tiles, 2, half, width), bf16),
            pltpu.VMEM((3, tiles, 2, half, width), bf16),
            pltpu.VMEM((3, tiles, 2, half, width), bf16),
            pltpu.VMEM((tiles, n, tiles, half, lanes), bf16),
            pltpu.VMEM((tiles, n, tiles, half, lanes), bf16),
            pltpu.VMEM((3, tiles + 2, half, lanes), bf16),
            pltpu.VMEM((2, half, lanes), bf16),
            pltpu.VMEM((tiles, lanes, width), f32),
            pltpu.VMEM((lanes, 2 * count), f32),
            pltpu.VMEM((n, 2, 2, share, count), f32),
            pltpu.VMEM((n, 2, 2, share, count), f32),
            dma((tiles,)),
            dma((n,)),
            dma((3, tiles)),
            dma((3, tiles)),
            dma((nf, tiles)),
            dma((nf, tiles)),
            dma((n, tiles)),
            dma((n, tiles)),
            dma((2,)),
            dma((2,)),
            dma((n,)),
            dma((n,)),
        ],
        compiler_params=pltpu.CompilerParams(
            collective_id=0, has_side_effects=True, vmem_limit_bytes=60 << 20
        ),
        name="reflection_operator",
    )(tile_ranks, spec, u_factors, v_factors)


def solution(mesh):
    placed = (
        P("freq", None, "tile"),
        P("freq", None, "tile"),
        P("freq", "tile"),
        P("freq", None, "tile"),
        P("freq", "tile", None, None, None, None),
        P("freq", None, "tile", None, None, None),
    )
    return jax.shard_map(
        functools.partial(on_device, mesh.shape["tile"], mesh.shape["freq"]),
        mesh=mesh,
        in_specs=placed,
        out_specs=(
            P("freq", None, None, "tile"),
            P("freq", None, None, "tile"),
            P("freq", None, "tile", None),
            P("freq", None, "tile", None),
        ),
        check_vma=False,
    )
```
